32 devices in a mesh: fiber: 8 (over z, x), seg: 4 (over y, core).
Axes of the slice: x: 2, y: 2, z: 4, core: 2. Of those that a mesh axis runs over, the one named last changes fastest.
Arguments:
- raw_strain: bfloat16 [64, 1024, 2048], P('seg', 'fiber'), may hold values from -6 to 6
- fir_taps: float32 [31], replicated, may hold values from -1 to 1
- good_mask: int32 [64, 1024], P('seg', 'fiber'), may hold values from 0 to 1, as said below
Outputs:
- stacked_spectra: float32 [144, 1024, 2, 128], P('seg', 'fiber')
The draws below stay inside these ranges and needn't reach their ends.
Inputs may be any that keep to these rules, and one draw needn't show every extreme that they name: `good_mask`: 0 or 1; some channels are 0 in every segment.
All inputs are finite; a program needn't handle non-finite values.
Results may differ from the reference program's by a relative error of at most 0.005.
Values may be sent and summed in bfloat16 or wider, within the bound.
A program may use at most 192 MiB of HBM per device.

```python
import math
import jax
import jax.numpy as jnp
from jax import lax

SAMPLES = 2048
NF = 144
LOW = 16
HALF = 15
TAPS = 31
SMOOTH = 4
LAGS = 128
CH_DEV = 128
NCH = 1024
SEGS = 64


def draw_good_mask(key, part):
    key_dead = jax.random.fold_in(key, 11)
    key_drop = jax.random.fold_in(key, 12)
    alive = jax.random.randint(key_dead, (1, NCH), 0, 16) != 0
    kept = jax.random.randint(key_drop, (SEGS, NCH), 0, 5) != 0
    return (alive & kept).astype(jnp.int32)


def block_levels(key, shape, pieces, least, largest):
    level, own = 1.0, jax.random.fold_in(key, 6)
    for axis_at, parts in pieces:
        draws = jnp.exp(jax.random.uniform(jax.random.fold_in(own, axis_at), (parts,), jnp.float32, least / len(pieces), largest / len(pieces)))
        level = level * jnp.repeat(draws, shape[axis_at] // parts).reshape([-1 if axis == axis_at else 1 for axis in range(len(shape))])
    return level


def gaussian(rng, shape, scale, limit, split=(), held_as=jnp.bfloat16):
    loudness = block_levels(rng, shape, split, -0.22, 0.18) if split else 1.0
    values = jax.random.normal(rng, shape, jnp.float32) * scale * loudness
    return jnp.minimum(jnp.maximum(values, -limit), limit).astype(held_as)


def setup_inputs(seed: int = 0) -> dict:
    seeds = jax.random.split(jax.random.key(seed), 4)
    return {
        "raw_strain": gaussian(seeds[0], (SEGS, NCH, SAMPLES), 1.0, 6.0, ((0, 4), (1, 8))),
        "fir_taps": jnp.clip(jax.random.uniform(seeds[1], (TAPS,), jnp.float32, -1.0, 1.0), -1.0, 1.0),
        "good_mask": draw_good_mask(jax.random.fold_in(seeds[3], 71), 0),
    }


epsilon = 1e-06
water_share = 0.1

def dft_basis(samples):
    times = jnp.arange(samples, dtype=jnp.int32)
    bins = jnp.arange(NF, dtype=jnp.int32) + LOW
    phase_index = times[:, None] * bins[None, :] % samples
    angles = phase_index.astype(jnp.float32) * (2.0 * math.pi / samples)
    return jnp.stack([jnp.cos(angles), -jnp.sin(angles)], axis=2).astype(jnp.bfloat16)

def lag_band(gram):
    lead = gram.shape[:-2]
    rows = gram.shape[-2]
    cols = gram.shape[-1]
    flat = gram.reshape(lead + (rows * cols,))
    padding = [(0, 0)] * len(lead) + [(0, rows)]
    flat = jnp.pad(flat, padding)
    skewed = flat.reshape(lead + (rows, cols + 1))
    return skewed[..., 1:1 + LAGS]

def whiten(filtered, good_mask):
    powers = filtered[:, :, 0] * filtered[:, :, 0] + filtered[:, :, 1] * filtered[:, :, 1]
    bin_count = powers.shape[1]
    padded = jnp.pad(powers, ((0, 0), (SMOOTH, SMOOTH), (0, 0)))
    smooth = padded[:, 0:bin_count]
    for offset in range(1, 2 * SMOOTH + 1):
        smooth = smooth + padded[:, offset:offset + bin_count]
    smooth = smooth / (2 * SMOOTH + 1)
    water_level = lax.optimization_barrier(jnp.mean(powers, axis=1, keepdims=True))
    divisor = jnp.sqrt(smooth + water_share * water_level + epsilon)
    scaled = good_mask.astype(jnp.float32)[:, None, :] / divisor
    return (filtered * scaled[:, :, None, :]).astype(jnp.bfloat16)

def cross_band(left_block, extended):
    rotated = jnp.stack([extended[:, :, 1], -extended[:, :, 0]], axis=2)
    gram_real = jnp.einsum('sfrc,sfrd->fcd', left_block, extended, precision=lax.Precision.HIGHEST)
    gram_imag = jnp.einsum('sfrc,sfrd->fcd', left_block, rotated, precision=lax.Precision.HIGHEST)
    return jnp.stack([lag_band(gram_real), lag_band(gram_imag)], axis=2)

def reference(raw_strain, fir_taps, good_mask):
    basis = dft_basis(SAMPLES).astype(jnp.float32)

    def one_segment(inputs):
        segment, segment_mask = inputs
        spectra = jnp.einsum('ct,tfr->frc', segment.astype(jnp.float32), basis, precision=lax.Precision.HIGHEST)
        padded = jnp.pad(spectra, ((0, 0), (0, 0), (HALF, HALF)))
        filtered = fir_taps[0] * padded[:, :, 0:NCH]
        for tap_index in range(1, 2 * HALF + 1):
            filtered = filtered + fir_taps[tap_index] * padded[:, :, tap_index:tap_index + NCH]
        return whiten(filtered[None], segment_mask[None])[0]
    whitened = lax.map(one_segment, (raw_strain, good_mask))
    padded_white = jnp.pad(whitened, ((0, 0), (0, 0), (0, 0), (0, CH_DEV)))
    mask_float = good_mask.astype(jnp.float32)
    padded_mask = jnp.pad(mask_float, ((0, 0), (0, CH_DEV)))

    def one_block(block_index):
        first = (block_index * CH_DEV).astype(jnp.int32)
        left_block = lax.dynamic_slice_in_dim(whitened, first, CH_DEV, 3).astype(jnp.float32)
        extended = lax.dynamic_slice_in_dim(padded_white, first, 2 * CH_DEV, 3).astype(jnp.float32)
        sums = cross_band(left_block, extended)
        mask_left = lax.dynamic_slice_in_dim(mask_float, first, CH_DEV, 1)
        mask_wide = lax.dynamic_slice_in_dim(padded_mask, first, 2 * CH_DEV, 1)
        counts = lag_band(jnp.einsum('sc,sd->cd', mask_left, mask_wide, precision=lax.Precision.HIGHEST))
        return sums / jnp.maximum(counts, 1.0)[None, :, None, :]
    blocks = lax.map(one_block, jnp.arange(NCH // CH_DEV, dtype=jnp.int32))
    return jnp.transpose(blocks, (1, 0, 2, 3, 4)).reshape(NF, NCH, 2, LAGS)
```

```python
import functools
import math

import jax
import jax.numpy as jnp
import numpy as np
from jax import lax
from jax.experimental import pallas as pl
from jax.experimental.pallas import tpu as pltpu
from jax.sharding import PartitionSpec as P

NF = 144
LOW = 16
SMOOTH = 4
LAGS = 128
EDGE = 16

epsilon = 1e-06
water_share = 0.1
MESH = pl.DeviceIdType.MESH
VMEM_LIMIT = 44 * 2**20
scope = jax.named_scope


def row_bins(shares):
    per = NF // shares
    return np.concatenate([np.tile(np.arange(k * per, (k + 1) * per), 2) for k in range(shares)])


def row_parts(shares):
    per = NF // shares
    return np.tile(np.repeat(np.arange(2), per), shares)


def dft_rows(samples, shares):
    bins, parts = row_bins(shares), row_parts(shares)
    index = ((bins[:, None] + LOW) * np.arange(samples)[None, :]) % samples
    angles = index.astype(np.float64) * (2.0 * math.pi / samples)
    return np.where(parts[:, None] == 0, np.cos(angles), -np.sin(angles)).astype(jnp.bfloat16)


def smooth_rows(shares):
    bins = row_bins(shares)
    return (np.abs(bins[:, None] - bins[None, :]) <= SMOOTH).astype(jnp.bfloat16)


def two_terms(x):
    hi = x.astype(jnp.bfloat16)
    return hi, (x - hi.astype(jnp.float32)).astype(jnp.bfloat16)


def mm(a, b):
    return jnp.dot(a, b, preferred_element_type=jnp.float32)


def mm_t(a, b):
    return lax.dot_general(a, b, (((1,), (1,)), ((), ())), preferred_element_type=jnp.float32)


def turned(x, shift):
    return pltpu.roll(x, shift, 1) if shift else x


def partner(seg, m):
    bit = 1
    while bit <= m:
        if m & bit:
            seg = seg + bit - 2 * bit * (seg // bit % 2)
        bit *= 2
    return seg


def taken(ref, part, q):
    blocks, _, _, size, channels = ref.shape
    return ref[:, part, q].reshape(blocks * size, channels)


def bin_groups(bins):
    unit = bins // 12
    sizes = [3 * unit, 3 * unit, 3 * unit, 2 * unit, unit] if bins % 12 == 0 else [bins]
    starts = [sum(sizes[:i]) for i in range(len(sizes))]
    return list(zip(starts, sizes))


def late_blocks(shares, chunks):
    blocks = [(chunks - 1, m) for m in range(1, shares) if 2 * m >= shares]
    return blocks + [(c, shares - 1) for c in range(chunks - 2, chunks - 1) if c >= 0]


def next_messages(shares, chunks, bins):
    late = late_blocks(shares, chunks)
    early = [(c, m) for c in range(chunks) for m in range(shares) if (c, m) not in late]
    return [(c, m, 0, bins, 0) for c, m in early] + [
        (c, m, lo, n, 1 + g) for g, (lo, n) in enumerate(bin_groups(bins)) for c, m in late
    ]


def right_side(ref, q):
    re, im = taken(ref, 0, q), taken(ref, 1, q)
    return jnp.concatenate(
        [jnp.concatenate([re, im], axis=1), jnp.concatenate([im, -re], axis=1)], axis=0
    )


def lagged(near, far):
    row = lax.broadcasted_iota(jnp.int32, near.shape, 0)
    col = lax.broadcasted_iota(jnp.int32, near.shape, 1)
    chosen = jnp.where(col > row, near, far)
    return jnp.take_along_axis(chosen, (col + row + 1) % near.shape[0], axis=1)


def cross_bin(f, next_ref, part_ref, turn_ref, scale_v, out_ref, at):
    channels = next_ref.shape[-1]
    far = mm(turn_ref[at], right_side(next_ref, f))
    for n in range(2):
        cells = slice(n * channels, (n + 1) * channels)
        out_ref[at, pl.ds(n, channels, 2), :] = (
            lagged(part_ref[at, :, cells], far[:, cells]) * scale_v[...]
        )


def each_bin(body, lo, count):
    group = next(n for n in (6, 4, 3, 2, 1) if count % n == 0)

    def step(i, carry):
        for b in range(group):
            body(lo + i * group + b)
        return carry

    lax.fori_loop(0, count // group, step, 0)


def spectra_kernel(
    fibers, shares, messages, taps_hbm, raw_ref, mask_ref, basis_hbm, smooth_hbm,
    out_ref, next_ref, part_tail, turn_tail, scale_v,
    own_ref, part_ref, turn_ref, own_flags, next_flags,
    taps_ref, raw_v, edge_v, basis_ref, smooth_ref, flag_v, spec_v, out_l, out_r, in_l, in_r, band_v, mask_v,
    white_v, send_v, send_flags,
    raw_sem, edge_sem, misc_sem, halo_send, halo_recv, own_send, own_recv, next_send, next_recv, local_sem,
    flag_sem,
):
    fib = lax.axis_index("fiber")
    seg = lax.axis_index("seg")
    segs, channels, _ = raw_ref.shape
    rows = basis_ref.shape[0]
    per = rows // shares
    bins = per // 2
    taps = taps_ref.shape[0]
    half = (taps - 1) // 2
    has_prev = fib > 0
    has_next = fib < fibers - 1
    prev = jnp.maximum(fib - 1, 0)
    following = jnp.minimum(fib + 1, fibers - 1)
    size = channels // EDGE
    chunks = segs // size
    groups = bin_groups(bins)
    pairs = segs // 2
    chunk_pairs = size // 2

    taps_copy = pltpu.make_async_copy(taps_hbm, taps_ref, misc_sem.at[3])
    taps_copy.start()
    basis_copy = pltpu.make_async_copy(basis_hbm, basis_ref, misc_sem.at[0])
    basis_copy.start()
    edge_copies = [
        [
            pltpu.make_async_copy(
                raw_ref.at[pl.ds(c * size, size), pl.ds(start, EDGE), :],
                edge_v.at[c, i], edge_sem.at[c],
            )
            for i, start in enumerate((0, channels - EDGE))
        ]
        for c in range(chunks)
    ]
    for copies in edge_copies:
        for copy in copies:
            copy.start()
    mask_copy = pltpu.make_async_copy(mask_ref, flag_v, misc_sem.at[2])
    mask_copy.start()
    smooth_copy = pltpu.make_async_copy(smooth_hbm, smooth_ref, misc_sem.at[1])
    raw_copies = [
        pltpu.make_async_copy(raw_ref.at[pl.ds(2 * p, 2)], raw_v.at[p], raw_sem.at[p])
        for p in range(pairs)
    ]

    barrier = pltpu.get_barrier_semaphore()
    for m in range(1, shares):
        pl.semaphore_signal(
            barrier, inc=1, device_id=(fib, partner(seg, m)), device_id_type=MESH
        )
    @pl.when(has_prev)
    def _():
        pl.semaphore_signal(barrier, inc=1, device_id=(fib - 1, seg), device_id_type=MESH)
    @pl.when(has_next)
    def _():
        pl.semaphore_signal(barrier, inc=1, device_id=(fib + 1, seg), device_id_type=MESH)

    row = lax.broadcasted_iota(jnp.int32, (2 * channels, channels), 0)
    col = lax.broadcasted_iota(jnp.int32, (2 * channels, channels), 1)
    left = row - channels - EDGE
    right = row - EDGE
    place = jnp.where(row < channels, row, jnp.where(left < 0, left, right))
    place = jnp.where(row < channels + 2 * EDGE, place, 8 * channels)
    tap = place - col + half
    band = jnp.zeros((2 * channels, channels), jnp.float32)
    taps_copy.wait()
    for j in range(taps):
        band = jnp.where(tap == j, taps_ref[j], band)
    band_hi, band_lo = two_terms(band)
    band_v[:, :channels] = band_hi
    band_v[:, channels:] = band_lo

    for copy in raw_copies[:chunk_pairs]:
        copy.start()
    smooth_copy.start()

    @pl.when(jnp.logical_not(has_prev))
    def _():
        in_l[...] = jnp.zeros_like(in_l)
    @pl.when(jnp.logical_not(has_next))
    def _():
        in_r[...] = jnp.zeros_like(in_r)
        next_flags[...] = jnp.zeros_like(next_flags)

    def transform_edges(c):
        pltpu.make_async_copy(edge_v.at[c], edge_v.at[c], edge_sem.at[c]).wait()
        ends = mm_t(basis_ref[...], edge_v[c].reshape(2 * channels, -1)).astype(jnp.bfloat16)
        out_l[c] = ends[:, :channels]
        out_r[c] = ends[:, channels:]

    to_prev = [
        pltpu.make_async_remote_copy(
            src_ref=out_l.at[c], dst_ref=in_r.at[c],
            send_sem=halo_send.at[0], recv_sem=halo_recv.at[0, c],
            device_id=(prev, seg), device_id_type=MESH,
        )
        for c in range(chunks)
    ]
    to_next = [
        pltpu.make_async_remote_copy(
            src_ref=out_r.at[c], dst_ref=in_l.at[c],
            send_sem=halo_send.at[1], recv_sem=halo_recv.at[1, c],
            device_id=(following, seg), device_id_type=MESH,
        )
        for c in range(chunks)
    ]
    def send_edges(c):
        @pl.when(has_prev)
        def _():
            to_prev[c].start()
        @pl.when(has_next)
        def _():
            to_next[c].start()

    def waiting_for(area, send_sem, recv_sem):
        return pltpu.make_async_remote_copy(
            src_ref=area, dst_ref=area, send_sem=send_sem, recv_sem=recv_sem,
            device_id=(prev, seg), device_id_type=MESH,
        )

    def flags_own(m):
        return pltpu.make_async_remote_copy(
            src_ref=send_flags, dst_ref=own_flags.at[seg],
            send_sem=flag_sem.at[0], recv_sem=flag_sem.at[1],
            device_id=(fib, partner(seg, m)), device_id_type=MESH,
        )

    all_flags = waiting_for(own_flags.at[pl.ds(0, shares - 1)], flag_sem.at[0], flag_sem.at[1])

    def flags_next():
        return pltpu.make_async_remote_copy(
            src_ref=own_flags, dst_ref=next_flags,
            send_sem=flag_sem.at[2], recv_sem=flag_sem.at[3],
            device_id=(prev, seg), device_id_type=MESH,
        )

    sides = (fib + fibers - 1) // fibers + (2 * fibers - 2 - fib) // fibers
    with scope("basiswait"):
        basis_copy.wait()
    for c in range(chunks):
        with scope(f"edges{c}"):
            transform_edges(c)
        if c == 0:
            with scope("barrier"):
                pl.semaphore_wait(barrier, shares - 1 + sides)
            send_edges(c)
    for copy in raw_copies[chunk_pairs:]:
        copy.start()

    mask_copy.wait()
    mask_v[...] = flag_v[...].astype(jnp.float32)
    send_flags[...] = mask_v[...].astype(jnp.bfloat16)
    own_flags[seg] = mask_v[...].astype(jnp.bfloat16)
    for m in range(1, shares):
        flags_own(m).start()

    lane = lax.broadcasted_iota(jnp.int32, (rows, channels), 1)

    def transform(p):
        raw_copies[p].wait()
        spec_v[p] = mm_t(basis_ref[...], raw_v[p].reshape(2 * channels, -1))

    def whiten_pair(c, i):
        p = c * chunk_pairs + i
        lefts = in_l[c].astype(jnp.float32)
        rights = in_r[c].astype(jnp.float32)
        parts = []
        for h in range(2):
            slot = 2 * i + h
            l_roll = (channels - slot * EDGE) % channels
            r_roll = (channels + EDGE - slot * EDGE) % channels
            edges = jnp.where(lane < EDGE, turned(lefts, l_roll), turned(rights, r_roll))
            hi, lo = two_terms(spec_v[p, :, h * channels : (h + 1) * channels])
            wide = mm(jnp.concatenate([hi, edges.astype(jnp.bfloat16)], axis=1), band_v[...])
            parts.append(
                wide[:, :channels] + wide[:, channels:] + mm(lo, band_v[:channels, :channels])
            )
        filtered = jnp.concatenate(parts, axis=1)
        power = filtered * filtered
        smooth = mm(smooth_ref[...], power.astype(jnp.bfloat16))
        total = jnp.sum(power, axis=0, keepdims=True)
        level = smooth * (1.0 / (2 * SMOOTH + 1)) + (total * (water_share / NF) + epsilon)
        good = jnp.concatenate(
            [mask_v[pl.ds(2 * p, 1), :], mask_v[pl.ds(2 * p + 1, 1), :]], axis=1
        )
        white = filtered * (lax.rsqrt(level) * good)
        white_v[pl.ds(2 * i, rows, size), :] = white[:, :channels]
        white_v[pl.ds(2 * i + 1, rows, size), :] = white[:, channels:]

    def whiten(c):
        for i in range(chunk_pairs):
            whiten_pair(c, i)
        for k in range(shares):
            send_v[c * shares + k] = (
                white_v[k * per * size : (k + 1) * per * size, :]
                .reshape(2, bins, size, channels)
                .astype(jnp.bfloat16)
            )

    def to_own(c, m):
        other = partner(seg, m)
        return pltpu.make_async_remote_copy(
            src_ref=send_v.at[c * shares + other], dst_ref=own_ref.at[c * shares + seg],
            send_sem=own_send.at[0], recv_sem=own_recv.at[c, m],
            device_id=(fib, other), device_id_type=MESH,
        )

    def from_own(c, m):
        other = partner(seg, m)
        return pltpu.make_async_remote_copy(
            src_ref=send_v.at[c * shares + other], dst_ref=own_ref.at[c * shares + other],
            send_sem=own_send.at[0], recv_sem=own_recv.at[c, m],
            device_id=(fib, other), device_id_type=MESH,
        )

    def hand_on(message):
        c, m, lo, count, k = message
        source = c * shares + partner(seg, m)
        block = send_v if m == 0 else own_ref
        return pltpu.make_async_remote_copy(
            src_ref=block.at[source, :, pl.ds(lo, count)],
            dst_ref=next_ref.at[source, :, pl.ds(lo, count)],
            send_sem=next_send.at[0], recv_sem=next_recv.at[k],
            device_id=(prev, seg), device_id_type=MESH,
        )

    def hand_all(*blocks):
        @pl.when(has_prev)
        def _():
            for message in messages:
                if message[:2] in blocks:
                    hand_on(message).start()

    def kept(c):
        mine = c * shares + seg
        return pltpu.make_async_copy(send_v.at[mine], own_ref.at[mine], local_sem.at[0])

    def give(c):
        for m in reversed(range(1, shares)):
            to_own(c, m).start()
        hand_all((c, 0))
        kept(c).start()

    def relay(*blocks):
        for c, m in blocks:
            from_own(c, m).wait_recv()
        hand_all(*blocks)

    def own_bin(f, part, turn, at):
        turned_left = jnp.concatenate([taken(own_ref, 0, f), taken(own_ref, 1, f)], axis=0).T
        turn[at] = turned_left
        part[at] = mm(turned_left, right_side(own_ref, f))

    def grams(a, b):
        return lax.dot_general(a, b, (((0,), (0,)), ((), ())), preferred_element_type=jnp.float32)

    smooth_copy.wait()
    for c in range(chunks):
        for i in range(chunk_pairs):
            with scope(f"transform{c}{i}"):
                transform(c * chunk_pairs + i)
            if c + 1 < chunks and i == 2:
                send_edges(c + 1)
            if c and i == chunk_pairs // 2:
                with scope(f"relayin{c}"):
                    relay((c - 1, 1))
        with scope(f"halowait{c}"):
            @pl.when(has_prev)
            def _():
                to_next[c].wait_recv()
            @pl.when(has_next)
            def _():
                to_prev[c].wait_recv()
        with scope(f"whiten{c}"):
            whiten(c)
        with scope(f"give{c}"):
            give(c)

    @pl.when(jnp.logical_not(has_next))
    def _():
        next_ref[...] = jnp.zeros_like(next_ref)

    with scope("flags"):
        all_flags.wait_recv()
        @pl.when(has_prev)
        def _():
            flags_next().start()

    late = late_blocks(shares, chunks)
    early = [(chunks - 1, 1)] + [(c, m) for c in range(chunks) for m in range(2, shares)]
    for c, m in early:
        if (c, m) not in late:
            with scope(f"relay{c}{m}"):
                relay((c, m))
    with scope("relaylate"):
        relay(*late)
    given = send_v.at[pl.ds(0, chunks)]
    pltpu.make_async_copy(given, given, local_sem.at[0]).wait()

    with scope("ownprod"):
        tail, count = groups[-1]
        each_bin(lambda f: own_bin(f, part_ref, turn_ref, f), 0, tail)
        for f in range(count):
            own_bin(tail + f, part_tail, turn_tail, f)

    with scope("scale"):
        @pl.when(has_next)
        def _():
            flags_next().wait_recv()
        here = own_flags[...].reshape(shares * segs, channels)
        there = next_flags[...].reshape(shares * segs, channels)
        scale_v[...] = 1.0 / jnp.maximum(lagged(grams(here, here), grams(here, there)), 1.0)

    for g, (lo, count) in enumerate(groups):
        with scope(f"recv{lo}"):
            @pl.when(has_next)
            def _():
                if g == 0:
                    whole = next_ref.at[pl.ds(0, shares * chunks - len(late))]
                    waiting_for(whole, next_send.at[0], next_recv.at[0]).wait_recv()
                area = next_ref.at[pl.ds(0, len(late)), :, pl.ds(lo, count)]
                waiting_for(area, next_send.at[0], next_recv.at[1 + g]).wait_recv()
        if g + 1 < len(groups):
            with scope(f"cross{lo}"):
                each_bin(
                    lambda f: cross_bin(f, next_ref, part_ref, turn_ref, scale_v, out_ref, f), lo, count
                )

    all_flags.wait_send()
    waiting_for(
        send_v.at[pl.ds(0, chunks * (shares - 1))], own_send.at[0], own_recv.at[0, 0]
    ).wait_send()
    @pl.when(has_prev)
    def _():
        flags_next().wait_send()
        waiting_for(out_l, halo_send.at[0], halo_recv.at[0, 0]).wait_send()
        waiting_for(own_ref, next_send.at[0], next_recv.at[0]).wait_send()
    @pl.when(has_next)
    def _():
        waiting_for(out_r, halo_send.at[1], halo_recv.at[1, 0]).wait_send()


def finish_kernel(done_ref, next_ref, part_tail, turn_tail, scale_v, out_ref, last_v, sem):
    bins = done_ref.shape[0]
    lo, count = bin_groups(bins)[-1]
    copies = [
        pltpu.make_async_copy(done_ref.at[pl.ds(a, n)], out_ref.at[pl.ds(a, n)], sem.at[i])
        for i, (a, n) in enumerate(bin_groups(bins)[:-1])
    ]
    for copy in copies:
        copy.start()
    for i in range(count):
        cross_bin(lo + i, next_ref, part_tail, turn_tail, scale_v, last_v, i)
    copies.append(
        pltpu.make_async_copy(last_v, out_ref.at[pl.ds(lo, count)], sem.at[len(copies)])
    )
    copies[-1].start()
    for copy in copies:
        copy.wait()


def on_device(raw_strain, fir_taps, good_mask):
    segs, channels, samples = raw_strain.shape
    fibers, shares = lax.axis_size("fiber"), lax.axis_size("seg")
    rows = 2 * NF
    per = rows // shares
    bins = per // 2
    size = channels // EDGE
    chunks = segs // size
    shape = (shares * chunks, 2, bins, size, channels)
    block = pltpu.VMEM(shape, jnp.bfloat16)
    flags = pltpu.VMEM((shares, segs, channels), jnp.bfloat16)
    vmem = pl.BlockSpec(memory_space=pltpu.VMEM)
    hbm = pl.BlockSpec(memory_space=pltpu.HBM)
    edges = pltpu.VMEM((chunks, rows, size * EDGE), jnp.bfloat16)
    basis, smooth = dft_rows(samples, shares), smooth_rows(shares)
    dma = pltpu.SemaphoreType.DMA
    messages = next_messages(shares, chunks, bins)
    count = bin_groups(bins)[-1][1]
    whole = jax.ShapeDtypeStruct((bins, 2 * channels, LAGS), jnp.float32)
    crossed = pl.pallas_call(
        functools.partial(spectra_kernel, fibers, shares, messages),
        out_shape=(
            whole,
            jax.ShapeDtypeStruct(shape, jnp.bfloat16),
            jax.ShapeDtypeStruct((count, channels, 2 * channels), jnp.float32),
            jax.ShapeDtypeStruct((count, channels, 2 * shares * segs), jnp.bfloat16),
            jax.ShapeDtypeStruct((channels, LAGS), jnp.float32),
        ),
        in_specs=[hbm] * 5,
        out_specs=(vmem,) * 5,
        scratch_shapes=[
            block,
            pltpu.VMEM((bins - count, channels, 2 * channels), jnp.float32),
            pltpu.VMEM((bins - count, channels, 2 * shares * segs), jnp.bfloat16),
            flags,
            flags,
            pltpu.SMEM(fir_taps.shape, jnp.float32),
            pltpu.VMEM((segs // 2, 2, channels, samples), jnp.bfloat16),
            pltpu.VMEM((chunks, 2, size, EDGE, samples), jnp.bfloat16),
            pltpu.VMEM(basis.shape, jnp.bfloat16),
            pltpu.VMEM(smooth.shape, jnp.bfloat16),
            pltpu.VMEM((segs, channels), jnp.int32),
            pltpu.VMEM((segs // 2, rows, 2 * channels), jnp.float32),
            edges, edges, edges, edges,
            pltpu.VMEM((2 * channels, 2 * channels), jnp.bfloat16),
            pltpu.VMEM((segs, channels), jnp.float32),
            pltpu.VMEM((rows * size, channels), jnp.float32),
            block,
            pltpu.VMEM((segs, channels), jnp.bfloat16),
            dma((segs // 2,)),
            dma((chunks,)),
            dma((4,)),
            dma((2,)),
            dma((2, chunks)),
            dma((1,)),
            dma((chunks, shares)),
            dma((1,)),
            dma((1 + len(bin_groups(bins)),)),
            dma((1,)),
            dma((4,)),
        ],
        compiler_params=pltpu.CompilerParams(
            collective_id=0, has_side_effects=True, vmem_limit_bytes=VMEM_LIMIT
        ),
        name="spectra",
    )(
        *(
            pltpu.with_memory_space_constraint(x, pltpu.HBM)
            for x in (fir_taps, raw_strain, good_mask, jnp.asarray(basis), jnp.asarray(smooth))
        ),
    )
    out = pl.pallas_call(
        finish_kernel,
        out_shape=whole,
        in_specs=[vmem] * 5,
        out_specs=hbm,
        scratch_shapes=[
            pltpu.VMEM((count, 2 * channels, LAGS), jnp.float32),
            dma((len(bin_groups(bins)),)),
        ],
        compiler_params=pltpu.CompilerParams(vmem_limit_bytes=VMEM_LIMIT),
        name="finish",
    )(*crossed)
    return out.reshape(bins, channels, 2, LAGS)


def solution(mesh):
    return jax.shard_map(
        on_device,
        mesh=mesh,
        in_specs=(P("seg", "fiber", None), P(), P("seg", "fiber")),
        out_specs=P("seg", "fiber", None, None),
        check_vma=False,
    )
```

```python
import functools
import math

import jax
import jax.numpy as jnp
import numpy as np
from jax import lax
from jax.experimental import pallas as pl
from jax.experimental.pallas import tpu as pltpu
from jax.sharding import PartitionSpec as P

NF = 144
LOW = 16
SMOOTH = 4
LAGS = 128
EDGE = 16

epsilon = 1e-06
water_share = 0.1
MESH = pl.DeviceIdType.MESH
VMEM_LIMIT = 44 * 2**20
scope = jax.named_scope


def row_bins(shares):
    per = NF // shares
    return np.concatenate([np.tile(np.arange(k * per, (k + 1) * per), 2) for k in range(shares)])


def row_parts(shares):
    per = NF // shares
    return np.tile(np.repeat(np.arange(2), per), shares)


def dft_rows(samples, shares):
    bins, parts = row_bins(shares), row_parts(shares)
    index = ((bins[:, None] + LOW) * np.arange(samples)[None, :]) % samples
    angles = index.astype(np.float64) * (2.0 * math.pi / samples)
    return np.where(parts[:, None] == 0, np.cos(angles), -np.sin(angles)).astype(jnp.bfloat16)


def smooth_rows(shares):
    bins = row_bins(shares)
    return (np.abs(bins[:, None] - bins[None, :]) <= SMOOTH).astype(jnp.bfloat16)


def two_terms(x):
    hi = x.astype(jnp.bfloat16)
    return hi, (x - hi.astype(jnp.float32)).astype(jnp.bfloat16)


def mm(a, b):
    return jnp.dot(a, b, preferred_element_type=jnp.float32)


def mm_t(a, b):
    return lax.dot_general(a, b, (((1,), (1,)), ((), ())), preferred_element_type=jnp.float32)


def turned(x, shift):
    return pltpu.roll(x, shift, 1) if shift else x


def partner(seg, m):
    bit = 1
    while bit <= m:
        if m & bit:
            seg = seg + bit - 2 * bit * (seg // bit % 2)
        bit *= 2
    return seg


def taken(ref, part, q):
    blocks, _, _, size, channels = ref.shape
    return ref[:, part, q].reshape(blocks * size, channels)


def bin_groups(bins):
    unit = bins // 12
    sizes = [3 * unit, 3 * unit, 3 * unit, 2 * unit, unit] if bins % 12 == 0 else [bins]
    starts = [sum(sizes[:i]) for i in range(len(sizes))]
    return list(zip(starts, sizes))


def late_blocks(shares, chunks):
    blocks = [(chunks - 1, m) for m in range(1, shares) if 2 * m >= shares]
    return blocks + [(c, shares - 1) for c in range(chunks - 2, chunks - 1) if c >= 0]


def next_messages(shares, chunks, bins):
    late = late_blocks(shares, chunks)
    early = [(c, m) for c in range(chunks) for m in range(shares) if (c, m) not in late]
    return [(c, m, 0, bins, 0) for c, m in early] + [
        (c, m, lo, n, 1 + g) for g, (lo, n) in enumerate(bin_groups(bins)) for c, m in late
    ]


def right_side(ref, q):
    re, im = taken(ref, 0, q), taken(ref, 1, q)
    return jnp.concatenate(
        [jnp.concatenate([re, im], axis=1), jnp.concatenate([im, -re], axis=1)], axis=0
    )


def lagged(near, far):
    row = lax.broadcasted_iota(jnp.int32, near.shape, 0)
    col = lax.broadcasted_iota(jnp.int32, near.shape, 1)
    chosen = jnp.where(col > row, near, far)
    return jnp.take_along_axis(chosen, (col + row + 1) % near.shape[0], axis=1)


def cross_bin(f, next_ref, part_ref, turn_ref, scale_v, out_ref, at):
    channels = next_ref.shape[-1]
    far = mm(turn_ref[at], right_side(next_ref, f))
    for n in range(2):
        cells = slice(n * channels, (n + 1) * channels)
        out_ref[at, pl.ds(n, channels, 2), :] = (
            lagged(part_ref[at, :, cells], far[:, cells]) * scale_v[...]
        )


def each_bin(body, lo, count):
    group = next(n for n in (6, 4, 3, 2, 1) if count % n == 0)

    def step(i, carry):
        for b in range(group):
            body(lo + i * group + b)
        return carry

    lax.fori_loop(0, count // group, step, 0)


def spectra_kernel(
    fibers, shares, messages, taps_hbm, raw_ref, mask_ref, basis_hbm, smooth_hbm,
    out_ref, next_ref, part_tail, turn_tail, scale_v,
    own_ref, part_ref, turn_ref, own_flags, next_flags,
    taps_ref, raw_v, edge_v, basis_ref, smooth_ref, flag_v, spec_v, out_l, out_r, in_l, in_r, band_v, ends_v, mask_v,
    white_v, send_v, send_flags,
    raw_sem, edge_sem, misc_sem, halo_send, halo_recv, own_send, own_recv, next_send, next_recv, local_sem,
    flag_sem,
):
    fib = lax.axis_index("fiber")
    seg = lax.axis_index("seg")
    segs, channels, _ = raw_ref.shape
    rows = basis_ref.shape[0]
    per = rows // shares
    bins = per // 2
    taps = taps_ref.shape[0]
    half = (taps - 1) // 2
    has_prev = fib > 0
    has_next = fib < fibers - 1
    prev = jnp.maximum(fib - 1, 0)
    following = jnp.minimum(fib + 1, fibers - 1)
    size = channels // EDGE
    chunks = segs // size
    groups = bin_groups(bins)
    pairs = segs // 2
    chunk_pairs = size // 2

    taps_copy = pltpu.make_async_copy(taps_hbm, taps_ref, misc_sem.at[3])
    taps_copy.start()
    basis_copy = pltpu.make_async_copy(basis_hbm, basis_ref, misc_sem.at[0])
    basis_copy.start()
    edge_copies = [
        [
            pltpu.make_async_copy(
                raw_ref.at[pl.ds(c * size, size), pl.ds(start, EDGE), :],
                edge_v.at[c, i], edge_sem.at[c],
            )
            for i, start in enumerate((0, channels - EDGE))
        ]
        for c in range(chunks)
    ]
    for copies in edge_copies:
        for copy in copies:
            copy.start()
    mask_copy = pltpu.make_async_copy(mask_ref, flag_v, misc_sem.at[2])
    mask_copy.start()
    smooth_copy = pltpu.make_async_copy(smooth_hbm, smooth_ref, misc_sem.at[1])
    raw_copies = [
        pltpu.make_async_copy(raw_ref.at[pl.ds(2 * p, 2)], raw_v.at[p], raw_sem.at[p])
        for p in range(pairs)
    ]

    barrier = pltpu.get_barrier_semaphore()
    for m in range(1, shares):
        pl.semaphore_signal(
            barrier, inc=1, device_id=(fib, partner(seg, m)), device_id_type=MESH
        )
    @pl.when(has_prev)
    def _():
        pl.semaphore_signal(barrier, inc=1, device_id=(fib - 1, seg), device_id_type=MESH)
    @pl.when(has_next)
    def _():
        pl.semaphore_signal(barrier, inc=1, device_id=(fib + 1, seg), device_id_type=MESH)

    row = lax.broadcasted_iota(jnp.int32, (2 * channels, channels), 0)
    col = lax.broadcasted_iota(jnp.int32, (2 * channels, channels), 1)
    left = row - channels - EDGE
    right = row - EDGE
    place = jnp.where(row < channels, row, jnp.where(left < 0, left, right))
    place = jnp.where(row < channels + 2 * EDGE, place, 8 * channels)
    tap = place - col + half
    band = jnp.zeros((2 * channels, channels), jnp.float32)
    taps_copy.wait()
    for j in range(taps):
        band = jnp.where(tap == j, taps_ref[j], band)
    band_hi, band_lo = two_terms(band)
    band_v[:channels, :channels] = band_hi[:channels]
    band_v[:channels, channels:] = band_lo[:channels]
    band_v[channels:, :channels] = band_hi[:channels]
    band_v[channels:, channels:] = jnp.zeros_like(band_lo[:channels])
    ends_v[:, :channels] = band_hi[channels:]
    ends_v[:, channels:] = band_lo[channels:]

    for copy in raw_copies[:chunk_pairs]:
        copy.start()
    smooth_copy.start()

    @pl.when(jnp.logical_not(has_prev))
    def _():
        in_l[...] = jnp.zeros_like(in_l)
    @pl.when(jnp.logical_not(has_next))
    def _():
        in_r[...] = jnp.zeros_like(in_r)
        next_flags[...] = jnp.zeros_like(next_flags)

    def transform_edges(c):
        pltpu.make_async_copy(edge_v.at[c], edge_v.at[c], edge_sem.at[c]).wait()
        ends = mm_t(basis_ref[...], edge_v[c].reshape(2 * channels, -1)).astype(jnp.bfloat16)
        out_l[c] = ends[:, :channels]
        out_r[c] = ends[:, channels:]

    to_prev = [
        pltpu.make_async_remote_copy(
            src_ref=out_l.at[c], dst_ref=in_r.at[c],
            send_sem=halo_send.at[0], recv_sem=halo_recv.at[0, c],
            device_id=(prev, seg), device_id_type=MESH,
        )
        for c in range(chunks)
    ]
    to_next = [
        pltpu.make_async_remote_copy(
            src_ref=out_r.at[c], dst_ref=in_l.at[c],
            send_sem=halo_send.at[1], recv_sem=halo_recv.at[1, c],
            device_id=(following, seg), device_id_type=MESH,
        )
        for c in range(chunks)
    ]
    def send_edges(c):
        @pl.when(has_prev)
        def _():
            to_prev[c].start()
        @pl.when(has_next)
        def _():
            to_next[c].start()

    def waiting_for(area, send_sem, recv_sem):
        return pltpu.make_async_remote_copy(
            src_ref=area, dst_ref=area, send_sem=send_sem, recv_sem=recv_sem,
            device_id=(prev, seg), device_id_type=MESH,
        )

    def flags_own(m):
        return pltpu.make_async_remote_copy(
            src_ref=send_flags, dst_ref=own_flags.at[seg],
            send_sem=flag_sem.at[0], recv_sem=flag_sem.at[1],
            device_id=(fib, partner(seg, m)), device_id_type=MESH,
        )

    all_flags = waiting_for(own_flags.at[pl.ds(0, shares - 1)], flag_sem.at[0], flag_sem.at[1])

    def flags_next():
        return pltpu.make_async_remote_copy(
            src_ref=own_flags, dst_ref=next_flags,
            send_sem=flag_sem.at[2], recv_sem=flag_sem.at[3],
            device_id=(prev, seg), device_id_type=MESH,
        )

    sides = (fib + fibers - 1) // fibers + (2 * fibers - 2 - fib) // fibers
    with scope("basiswait"):
        basis_copy.wait()
    for c in range(chunks):
        with scope(f"edges{c}"):
            transform_edges(c)
        if c == 0:
            with scope("barrier"):
                pl.semaphore_wait(barrier, shares - 1 + sides)
            send_edges(c)
    for copy in raw_copies[chunk_pairs:]:
        copy.start()

    mask_copy.wait()
    mask_v[...] = flag_v[...].astype(jnp.float32)
    send_flags[...] = mask_v[...].astype(jnp.bfloat16)
    own_flags[seg] = mask_v[...].astype(jnp.bfloat16)
    for m in range(1, shares):
        flags_own(m).start()

    lane = lax.broadcasted_iota(jnp.int32, (rows, channels), 1)

    def transform(p):
        raw_copies[p].wait()
        spec_v[p] = mm_t(basis_ref[...], raw_v[p].reshape(2 * channels, -1))

    def filter_pair(p):
        for h in range(2):
            cells = slice(h * channels, (h + 1) * channels)
            wide = mm(jnp.concatenate(two_terms(spec_v[p, :, cells]), axis=1), band_v[...])
            spec_v[p, :, cells] = wide[:, :channels] + wide[:, channels:]

    def whiten_pair(c, i):
        p = c * chunk_pairs + i
        lefts = in_l[c].astype(jnp.float32)
        rights = in_r[c].astype(jnp.float32)
        parts = []
        for h in range(2):
            slot = 2 * i + h
            l_roll = (channels - slot * EDGE) % channels
            r_roll = (channels + EDGE - slot * EDGE) % channels
            edges = jnp.where(lane < EDGE, turned(lefts, l_roll), turned(rights, r_roll))
            wide = mm(edges.astype(jnp.bfloat16), ends_v[...])
            inner = spec_v[p, :, h * channels : (h + 1) * channels]
            parts.append(inner + (wide[:, :channels] + wide[:, channels:]))
        filtered = jnp.concatenate(parts, axis=1)
        power = filtered * filtered
        smooth = mm(smooth_ref[...], power.astype(jnp.bfloat16))
        total = jnp.sum(power, axis=0, keepdims=True)
        level = smooth * (1.0 / (2 * SMOOTH + 1)) + (total * (water_share / NF) + epsilon)
        good = jnp.concatenate(
            [mask_v[pl.ds(2 * p, 1), :], mask_v[pl.ds(2 * p + 1, 1), :]], axis=1
        )
        white = filtered * (lax.rsqrt(level) * good)
        white_v[pl.ds(2 * i, rows, size), :] = white[:, :channels]
        white_v[pl.ds(2 * i + 1, rows, size), :] = white[:, channels:]

    def whiten(c):
        for i in range(chunk_pairs):
            whiten_pair(c, i)
        for k in range(shares):
            send_v[c * shares + k] = (
                white_v[k * per * size : (k + 1) * per * size, :]
                .reshape(2, bins, size, channels)
                .astype(jnp.bfloat16)
            )

    def to_own(c, m):
        other = partner(seg, m)
        return pltpu.make_async_remote_copy(
            src_ref=send_v.at[c * shares + other], dst_ref=own_ref.at[c * shares + seg],
            send_sem=own_send.at[0], recv_sem=own_recv.at[c, m],
            device_id=(fib, other), device_id_type=MESH,
        )

    def from_own(c, m):
        other = partner(seg, m)
        return pltpu.make_async_remote_copy(
            src_ref=send_v.at[c * shares + other], dst_ref=own_ref.at[c * shares + other],
            send_sem=own_send.at[0], recv_sem=own_recv.at[c, m],
            device_id=(fib, other), device_id_type=MESH,
        )

    def hand_on(message):
        c, m, lo, count, k = message
        source = c * shares + partner(seg, m)
        block = send_v if m == 0 else own_ref
        return pltpu.make_async_remote_copy(
            src_ref=block.at[source, :, pl.ds(lo, count)],
            dst_ref=next_ref.at[source, :, pl.ds(lo, count)],
            send_sem=next_send.at[0], recv_sem=next_recv.at[k],
            device_id=(prev, seg), device_id_type=MESH,
        )

    def hand_all(*blocks):
        @pl.when(has_prev)
        def _():
            for message in messages:
                if message[:2] in blocks:
                    hand_on(message).start()

    def kept(c):
        mine = c * shares + seg
        return pltpu.make_async_copy(send_v.at[mine], own_ref.at[mine], local_sem.at[0])

    def give(c):
        for m in reversed(range(1, shares)):
            to_own(c, m).start()
        hand_all((c, 0))
        kept(c).start()

    def relay(*blocks):
        for c, m in blocks:
            from_own(c, m).wait_recv()
        hand_all(*blocks)

    def own_bin(f, part, turn, at):
        turned_left = jnp.concatenate([taken(own_ref, 0, f), taken(own_ref, 1, f)], axis=0).T
        turn[at] = turned_left
        part[at] = mm(turned_left, right_side(own_ref, f))

    def grams(a, b):
        return lax.dot_general(a, b, (((0,), (0,)), ((), ())), preferred_element_type=jnp.float32)

    smooth_copy.wait()
    for c in range(chunks):
        for i in range(chunk_pairs):
            with scope(f"transform{c}{i}"):
                transform(c * chunk_pairs + i)
            if c + 1 < chunks and i == 2:
                send_edges(c + 1)
            if c and i == chunk_pairs // 2:
                with scope(f"relayin{c}"):
                    relay((c - 1, 1))
        with scope(f"filter{c}"):
            for i in range(chunk_pairs):
                filter_pair(c * chunk_pairs + i)
        with scope(f"halowait{c}"):
            @pl.when(has_prev)
            def _():
                to_next[c].wait_recv()
            @pl.when(has_next)
            def _():
                to_prev[c].wait_recv()
        with scope(f"whiten{c}"):
            whiten(c)
        with scope(f"give{c}"):
            give(c)

    @pl.when(jnp.logical_not(has_next))
    def _():
        next_ref[...] = jnp.zeros_like(next_ref)

    with scope("flags"):
        all_flags.wait_recv()
        @pl.when(has_prev)
        def _():
            flags_next().start()

    late = late_blocks(shares, chunks)
    early = [(chunks - 1, 1)] + [(c, m) for c in range(chunks) for m in range(2, shares)]
    for c, m in early:
        if (c, m) not in late:
            with scope(f"relay{c}{m}"):
                relay((c, m))
    with scope("relaylate"):
        relay(*late)
    given = send_v.at[pl.ds(0, chunks)]
    pltpu.make_async_copy(given, given, local_sem.at[0]).wait()

    with scope("ownprod"):
        tail, count = groups[-1]
        each_bin(lambda f: own_bin(f, part_ref, turn_ref, f), 0, tail)
        for f in range(count):
            own_bin(tail + f, part_tail, turn_tail, f)

    with scope("scale"):
        @pl.when(has_next)
        def _():
            flags_next().wait_recv()
        here = own_flags[...].reshape(shares * segs, channels)
        there = next_flags[...].reshape(shares * segs, channels)
        scale_v[...] = 1.0 / jnp.maximum(lagged(grams(here, here), grams(here, there)), 1.0)

    for g, (lo, count) in enumerate(groups):
        with scope(f"recv{lo}"):
            @pl.when(has_next)
            def _():
                if g == 0:
                    whole = next_ref.at[pl.ds(0, shares * chunks - len(late))]
                    waiting_for(whole, next_send.at[0], next_recv.at[0]).wait_recv()
                area = next_ref.at[pl.ds(0, len(late)), :, pl.ds(lo, count)]
                waiting_for(area, next_send.at[0], next_recv.at[1 + g]).wait_recv()
        if g + 1 < len(groups):
            with scope(f"cross{lo}"):
                each_bin(
                    lambda f: cross_bin(f, next_ref, part_ref, turn_ref, scale_v, out_ref, f), lo, count
                )

    all_flags.wait_send()
    waiting_for(
        send_v.at[pl.ds(0, chunks * (shares - 1))], own_send.at[0], own_recv.at[0, 0]
    ).wait_send()
    @pl.when(has_prev)
    def _():
        flags_next().wait_send()
        waiting_for(out_l, halo_send.at[0], halo_recv.at[0, 0]).wait_send()
        waiting_for(own_ref, next_send.at[0], next_recv.at[0]).wait_send()
    @pl.when(has_next)
    def _():
        waiting_for(out_r, halo_send.at[1], halo_recv.at[1, 0]).wait_send()


def finish_kernel(done_ref, next_ref, part_tail, turn_tail, scale_v, out_ref, last_v, sem):
    bins = done_ref.shape[0]
    lo, count = bin_groups(bins)[-1]
    copies = [
        pltpu.make_async_copy(done_ref.at[pl.ds(a, n)], out_ref.at[pl.ds(a, n)], sem.at[i])
        for i, (a, n) in enumerate(bin_groups(bins)[:-1])
    ]
    for copy in copies:
        copy.start()
    for i in range(count):
        cross_bin(lo + i, next_ref, part_tail, turn_tail, scale_v, last_v, i)
    copies.append(
        pltpu.make_async_copy(last_v, out_ref.at[pl.ds(lo, count)], sem.at[len(copies)])
    )
    copies[-1].start()
    for copy in copies:
        copy.wait()


def on_device(raw_strain, fir_taps, good_mask):
    segs, channels, samples = raw_strain.shape
    fibers, shares = lax.axis_size("fiber"), lax.axis_size("seg")
    rows = 2 * NF
    per = rows // shares
    bins = per // 2
    size = channels // EDGE
    chunks = segs // size
    shape = (shares * chunks, 2, bins, size, channels)
    block = pltpu.VMEM(shape, jnp.bfloat16)
    flags = pltpu.VMEM((shares, segs, channels), jnp.bfloat16)
    vmem = pl.BlockSpec(memory_space=pltpu.VMEM)
    hbm = pl.BlockSpec(memory_space=pltpu.HBM)
    edges = pltpu.VMEM((chunks, rows, size * EDGE), jnp.bfloat16)
    basis, smooth = dft_rows(samples, shares), smooth_rows(shares)
    dma = pltpu.SemaphoreType.DMA
    messages = next_messages(shares, chunks, bins)
    count = bin_groups(bins)[-1][1]
    whole = jax.ShapeDtypeStruct((bins, 2 * channels, LAGS), jnp.float32)
    crossed = pl.pallas_call(
        functools.partial(spectra_kernel, fibers, shares, messages),
        out_shape=(
            whole,
            jax.ShapeDtypeStruct(shape, jnp.bfloat16),
            jax.ShapeDtypeStruct((count, channels, 2 * channels), jnp.float32),
            jax.ShapeDtypeStruct((count, channels, 2 * shares * segs), jnp.bfloat16),
            jax.ShapeDtypeStruct((channels, LAGS), jnp.float32),
        ),
        in_specs=[hbm] * 5,
        out_specs=(vmem,) * 5,
        scratch_shapes=[
            block,
            pltpu.VMEM((bins - count, channels, 2 * channels), jnp.float32),
            pltpu.VMEM((bins - count, channels, 2 * shares * segs), jnp.bfloat16),
            flags,
            flags,
            pltpu.SMEM(fir_taps.shape, jnp.float32),
            pltpu.VMEM((segs // 2, 2, channels, samples), jnp.bfloat16),
            pltpu.VMEM((chunks, 2, size, EDGE, samples), jnp.bfloat16),
            pltpu.VMEM(basis.shape, jnp.bfloat16),
            pltpu.VMEM(smooth.shape, jnp.bfloat16),
            pltpu.VMEM((segs, channels), jnp.int32),
            pltpu.VMEM((segs // 2, rows, 2 * channels), jnp.float32),
            edges, edges, edges, edges,
            pltpu.VMEM((2 * channels, 2 * channels), jnp.bfloat16),
            pltpu.VMEM((channels, 2 * channels), jnp.bfloat16),
            pltpu.VMEM((segs, channels), jnp.float32),
            pltpu.VMEM((rows * size, channels), jnp.float32),
            block,
            pltpu.VMEM((segs, channels), jnp.bfloat16),
            dma((segs // 2,)),
            dma((chunks,)),
            dma((4,)),
            dma((2,)),
            dma((2, chunks)),
            dma((1,)),
            dma((chunks, shares)),
            dma((1,)),
            dma((1 + len(bin_groups(bins)),)),
            dma((1,)),
            dma((4,)),
        ],
        compiler_params=pltpu.CompilerParams(
            collective_id=0, has_side_effects=True, vmem_limit_bytes=VMEM_LIMIT
        ),
        name="spectra",
    )(
        *(
            pltpu.with_memory_space_constraint(x, pltpu.HBM)
            for x in (fir_taps, raw_strain, good_mask, jnp.asarray(basis), jnp.asarray(smooth))
        ),
    )
    out = pl.pallas_call(
        finish_kernel,
        out_shape=whole,
        in_specs=[vmem] * 5,
        out_specs=hbm,
        scratch_shapes=[
            pltpu.VMEM((count, 2 * channels, LAGS), jnp.float32),
            dma((len(bin_groups(bins)),)),
        ],
        compiler_params=pltpu.CompilerParams(vmem_limit_bytes=VMEM_LIMIT),
        name="finish",
    )(*crossed)
    return out.reshape(bins, channels, 2, LAGS)


def solution(mesh):
    return jax.shard_map(
        on_device,
        mesh=mesh,
        in_specs=(P("seg", "fiber", None), P(), P("seg", "fiber")),
        out_specs=P("seg", "fiber", None, None),
        check_vma=False,
    )
```
